32 devices in a mesh: head: 2 (over y), inner: 4 (over x, core), outer: 4 (over z).
Axes of the slice: x: 2, y: 2, z: 4, core: 2. Of those that a mesh axis runs over, the one named last changes fastest.
Arguments:
- queries: bfloat16 [16, 128, 4096], P(('inner', 'outer'), None, 'head'), may hold values from -2.5 to 2.5
- keys: bfloat16 [16, 128, 512], P(('inner', 'outer'), None, 'head'), may hold values from -2.5 to 2.5
- values: bfloat16 [16, 128, 512], P(('inner', 'outer'), None, 'head'), may hold values from -4 to 4
- grad_out: bfloat16 [16, 128, 4096], P(('inner', 'outer'), None, 'head'), may hold values from -4 to 4
- log_denominator: float32 [16, 128, 32], P(('inner', 'outer'), None, 'head'), may hold values from 6 to 9
- output_row_dot: float32 [16, 128, 32], P(('inner', 'outer'), None, 'head'), may hold values from -32 to 32
- offsets: int32 [16, 2], replicated, may hold values from 0 to 1984, as said below
Outputs:
- grad_query: bfloat16 [16, 128, 4096], P(('inner', 'outer'), 'head')
- grad_key: bfloat16 [16, 128, 512], P(('inner', 'outer'), 'head')
- grad_value: bfloat16 [16, 128, 512], P(('inner', 'outer'), 'head')
The draws below stay inside these ranges and needn't reach their ends.
Inputs may be any that keep to these rules, and one draw needn't show every extreme that they name: `offsets`: row b holds p * 64 and (31 - p) * 64, where p runs over a permutation of 0 to 15, so that all blocks' positions together are 0 to 2047, each once.
All inputs are finite; a program needn't handle non-finite values.
Results may differ from the reference program's by a relative error of at most 0.0058.
Values may be sent and summed in bfloat16 or wider, within the bound.
No kernel may reach another device: no remote copies, remote signals or barrier semaphores. Data moves between devices by JAX's collectives and lax.ppermute only.
A program may use at most 64 MiB of HBM per device.

```python
import math
import jax
import jax.numpy as jnp
from jax import lax

HEAD_WIDTH = 128
QUERY_HEADS = 32
KEY_VALUE_HEADS = 4
BLOCK_TOKENS = 128
INNER_STEPS = 3
OUTER_STEPS = 2
SEQUENCE_BLOCKS = 16
N_INNER = 4
N_OUTER = 4


def draw_offsets(key, part):
    halfway = BLOCK_TOKENS // 2
    order_drawn = jax.random.permutation(jax.random.fold_in(key, 11), SEQUENCE_BLOCKS).astype(jnp.int32)
    early = order_drawn * halfway
    late = (2 * SEQUENCE_BLOCKS - 1 - order_drawn) * halfway
    return jnp.stack([early, late], axis=1).astype(jnp.int32)


def block_scale(key, shape, pieces, least, high):
    level = 1.0
    for dim, blocks in pieces:
        draws = jax.random.uniform(jax.random.fold_in(jax.random.fold_in(key, 6), dim), (blocks,), jnp.float32, least / len(pieces), high / len(pieces))
        level = level * jnp.repeat(jnp.exp(draws), shape[dim] // blocks).reshape((-1,) + (1,) * (len(shape) - 1 - dim))
    return level


def scatter_about(own_key, dims, spread, limit, split=(), held_as=jnp.bfloat16):
    result = spread * jax.random.normal(own_key, dims, jnp.float32)
    if split:
        result = result * block_scale(own_key, dims, split, -0.22, 0.18)
    return jnp.clip(result, -limit, limit).astype(held_as)


def setup_inputs(seed: int = 0) -> dict:
    splits = jax.random.split(jax.random.key(seed), 8)
    queries = scatter_about(splits[0], (SEQUENCE_BLOCKS, BLOCK_TOKENS, QUERY_HEADS * HEAD_WIDTH), 1.0, 2.5, ((0, 16), (2, 2)))
    keys = scatter_about(splits[1], (SEQUENCE_BLOCKS, BLOCK_TOKENS, KEY_VALUE_HEADS * HEAD_WIDTH), 1.0, 2.5, ((0, 16), (2, 2)))
    values = scatter_about(splits[2], (SEQUENCE_BLOCKS, BLOCK_TOKENS, KEY_VALUE_HEADS * HEAD_WIDTH), 1.0, 4.0, ((0, 16), (2, 2)))
    grad_out = scatter_about(splits[3], (SEQUENCE_BLOCKS, BLOCK_TOKENS, QUERY_HEADS * HEAD_WIDTH), 1.0, 4.0, ((0, 16), (2, 2)))
    log_denominator = jnp.clip(6.0 + 3.0 * jax.random.uniform(splits[4], (SEQUENCE_BLOCKS, BLOCK_TOKENS, QUERY_HEADS), jnp.float32) ** block_scale(splits[4], (SEQUENCE_BLOCKS, BLOCK_TOKENS, QUERY_HEADS), ((0, 16), (2, 2)), -0.2, 0.2), 6.0, 9.0)
    output_row_dot = scatter_about(splits[5], (SEQUENCE_BLOCKS, BLOCK_TOKENS, QUERY_HEADS), 8.0, 32.0, ((0, 16), (2, 2)), jnp.float32)
    offsets = draw_offsets(jax.random.fold_in(splits[7], 71), 0)
    return dict(queries=queries, keys=keys, values=values, grad_out=grad_out, log_denominator=log_denominator, output_row_dot=output_row_dot, offsets=offsets)


def block_positions(offsets, tokens_per_block):
    halfway = tokens_per_block // 2
    within = jnp.arange(tokens_per_block, dtype=jnp.int32)
    starts = jnp.where(within[None, :] < halfway, offsets[:, 0:1], offsets[:, 1:2])
    return (starts + (within % halfway)[None, :]).astype(jnp.int32)

def rounded(numbers):
    return lax.optimization_barrier(numbers.astype(jnp.bfloat16)).astype(jnp.float32)

def pair_grads(packed):
    query_heads, grad_heads, norm_heads, dot_heads, query_pos, key_heads, value_heads, key_pos = packed
    scaling = 1.0 / math.sqrt(HEAD_WIDTH)
    query_float = query_heads.astype(jnp.float32)
    grad_float = grad_heads.astype(jnp.float32)
    key_float = key_heads.astype(jnp.float32)
    value_float = value_heads.astype(jnp.float32)
    scores = jnp.einsum('otgjd,ougd->ogjtu', query_float, key_float) * scaling
    visible = key_pos[:, None, None, None, :] <= query_pos[:, None, None, :, None]
    probabilities = jnp.where(visible, jnp.exp(scores - norm_heads[..., None]), 0.0)
    grad_probs = jnp.einsum('otgjd,ougd->ogjtu', grad_float, value_float)
    grad_scores = probabilities * (grad_probs - dot_heads[..., None])
    probs_low = rounded(probabilities)
    scores_low = rounded(grad_scores)
    grad_value = jnp.einsum('ogjtu,otgjd->ougd', probs_low, grad_float)
    grad_key = scaling * jnp.einsum('ogjtu,otgjd->ougd', scores_low, query_float)
    grad_query = scaling * jnp.einsum('ogjtu,ougd->otgjd', scores_low, key_float)
    return (grad_query, grad_key, grad_value)

def reference(queries, keys, values, grad_out, log_denominator, output_row_dot, offsets):
    blocks_all, tokens_per_block, query_cols = queries.shape
    heads_per_group = QUERY_HEADS // KEY_VALUE_HEADS
    query_layout = (N_INNER, N_OUTER, tokens_per_block, KEY_VALUE_HEADS, heads_per_group, HEAD_WIDTH)
    key_layout = (N_INNER, N_OUTER, tokens_per_block, KEY_VALUE_HEADS, HEAD_WIDTH)
    query_all = queries.reshape(query_layout)
    grad_all = grad_out.reshape(query_layout)
    key_all = keys.reshape(key_layout)
    value_all = values.reshape(key_layout)
    log_norm_full = jnp.transpose(log_denominator.reshape(N_INNER, N_OUTER, tokens_per_block, KEY_VALUE_HEADS, heads_per_group), (0, 1, 3, 4, 2))
    row_dot_full = jnp.transpose(output_row_dot.reshape(N_INNER, N_OUTER, tokens_per_block, KEY_VALUE_HEADS, heads_per_group), (0, 1, 3, 4, 2))
    position_all = block_positions(offsets, tokens_per_block).reshape(N_INNER, N_OUTER, tokens_per_block)
    grad_query = jnp.zeros(query_layout, jnp.float32)
    grad_key = jnp.zeros(key_layout, jnp.float32)
    grad_value = jnp.zeros(key_layout, jnp.float32)
    for inner_step in range(INNER_STEPS):
        for outer_step in range(OUTER_STEPS):
            key_here = jnp.roll(key_all, (inner_step, outer_step), axis=(0, 1))
            value_here = jnp.roll(value_all, (inner_step, outer_step), axis=(0, 1))
            pos_here = jnp.roll(position_all, (inner_step, outer_step), axis=(0, 1))
            term_query, term_key, term_value = lax.map(pair_grads, (query_all, grad_all, log_norm_full, row_dot_full, position_all, key_here, value_here, pos_here))
            grad_query = grad_query + term_query
            grad_key = grad_key + jnp.roll(term_key, (-inner_step, -outer_step), axis=(0, 1))
            grad_value = grad_value + jnp.roll(term_value, (-inner_step, -outer_step), axis=(0, 1))
    key_value_columns = KEY_VALUE_HEADS * HEAD_WIDTH
    return (grad_query.astype(jnp.bfloat16).reshape(blocks_all, tokens_per_block, query_cols), grad_key.astype(jnp.bfloat16).reshape(blocks_all, tokens_per_block, key_value_columns), grad_value.astype(jnp.bfloat16).reshape(blocks_all, tokens_per_block, key_value_columns))
```

```python
import math

import jax
import jax.numpy as jnp
from jax import lax
from jax.experimental import pallas as pl
from jax.experimental.pallas import tpu as pltpu
from jax.sharding import PartitionSpec as P

HEAD_WIDTH = 128
QUERY_HEADS = 32
KEY_VALUE_HEADS = 4
FAR = 2
BACK = 1

SCALE = 1.0 / math.sqrt(HEAD_WIDTH)
VMEM = pl.BlockSpec(memory_space=pltpu.VMEM)
SMEM = pl.BlockSpec(memory_space=pltpu.SMEM)
F32 = jnp.float32
BF16 = jnp.bfloat16
VMEM_LIMIT = 24 * 1024 * 1024


def dot_nt(a, b):
    return lax.dot_general(a, b, (((1,), (1,)), ((), ())), preferred_element_type=F32)


def dot_nn(a, b):
    return lax.dot_general(a, b, (((1,), (0,)), ((), ())), preferred_element_type=F32)


def call(kernel, name, out_shape, in_specs, *, flops=0, bytes_accessed=0, aliases=None, scratch=()):
    return pl.pallas_call(
        kernel,
        name=name,
        out_shape=out_shape,
        in_specs=in_specs,
        out_specs=jax.tree.map(lambda _: VMEM, out_shape),
        scratch_shapes=scratch,
        input_output_aliases=aliases or {},
        cost_estimate=pl.CostEstimate(flops=flops, bytes_accessed=bytes_accessed, transcendentals=0),
        compiler_params=pltpu.CompilerParams(vmem_limit_bytes=VMEM_LIMIT),
    )


def prep_kernel(k_ref, v_ref, norm_ref, dot_ref, kv_ref, rows_ref):
    kv_ref[0] = k_ref[...]
    kv_ref[1] = v_ref[...]
    tokens = norm_ref.shape[1]
    half = tokens // 2
    pairs = norm_ref.shape[0] // 2
    lanes = lax.broadcasted_iota(jnp.int32, (pairs, tokens), 1)
    for at, ref in enumerate((norm_ref, dot_ref)):
        even = ref[pl.ds(0, pairs, stride=2), :]
        odd = ref[pl.ds(1, pairs, stride=2), :]
        rows_ref[at, 0] = jnp.where(lanes < half, even, pltpu.roll(odd, half, 1))
        rows_ref[at, 1] = jnp.where(lanes < half, pltpu.roll(even, half, 1), odd)


def quadrant(query, kv_ref, slot, key_half, query_half, diagonal, first, sums_ref):
    q_ref, do_ref, rows_ref, dq_ref = query
    tokens = q_ref.shape[0]
    half = tokens // 2
    heads_kv = kv_ref.shape[-1] // HEAD_WIDTH
    per_group = q_ref.shape[1] // HEAD_WIDTH // heads_kv
    chunk = 4
    def rows_of(which):
        if isinstance(which, int):
            return pl.ds(which * half, half)
        return pl.ds(pl.multiple_of(which * half, half), half)

    key_rows, query_rows = rows_of(key_half), rows_of(query_half)
    if diagonal:
        u = lax.broadcasted_iota(jnp.int32, (half, chunk * half), 0)
        t = lax.broadcasted_iota(jnp.int32, (half, chunk * half), 1) % half
        visible = u <= t
    for g in range(heads_kv):
        cols = slice(g * HEAD_WIDTH, (g + 1) * HEAD_WIDTH)
        k = kv_ref[0, key_rows, cols]
        v = kv_ref[1, key_rows, cols]
        kt = k.T
        dk = dv = None
        for c in range(per_group // chunk):
            heads = [g * per_group + c * chunk + j for j in range(chunk)]
            qc = jnp.concatenate([q_ref[query_rows, h * HEAD_WIDTH : (h + 1) * HEAD_WIDTH] for h in heads], 0)
            doc = jnp.concatenate([do_ref[query_rows, h * HEAD_WIDTH : (h + 1) * HEAD_WIDTH] for h in heads], 0)
            pair = heads[0] // 2
            norm = jnp.concatenate([rows_ref[0, query_half, pl.ds(pair + i, 1), :] for i in range(chunk // 2)], 1)
            dots = jnp.concatenate([rows_ref[1, query_half, pl.ds(pair + i, 1), :] for i in range(chunk // 2)], 1)
            prob = jnp.exp(dot_nt(k, qc) * SCALE - norm)
            if diagonal:
                prob = jnp.where(visible, prob, 0.0)
            grad = prob * (dot_nt(v, doc) - dots)
            prob_low = prob.astype(BF16)
            grad_low = grad.astype(BF16)
            dv_c = dot_nn(prob_low, doc)
            dk_c = dot_nn(grad_low, qc)
            dv = dv_c if dv is None else dv + dv_c
            dk = dk_c if dk is None else dk + dk_c
            dq = dot_nn(kt, grad_low)
            for i in range(chunk // 2):
                part = dq[:, i * tokens : (i + 1) * tokens]
                if first:
                    dq_ref[query_half, pair + i] = part
                else:
                    dq_ref[query_half, pair + i] += part
        sums_ref[slot, 0, key_rows, cols] += dk
        sums_ref[slot, 1, key_rows, cols] += dv


def wrapped(index, steps, count):
    moved = index - steps
    return jnp.where(moved < 0, moved + count, moved)


def visit(off_ref, mine, other, kv_ref, sums_ref, slot, inner_back, outer_back, own):
    inner_count, outer_count = lax.axis_size("inner"), lax.axis_size("outer")
    i, o = lax.axis_index("inner"), lax.axis_index("outer")
    odd = i & 1
    key_block = wrapped(i, inner_back, inner_count) * outer_count + wrapped(o, outer_back, outer_count)
    key_start = off_ref[key_block, 0]

    def full(query, block, first):
        which = jnp.where(key_start < off_ref[block, 0], 0, 1)
        quadrant(query, kv_ref, slot, 0, 1, False, first, sums_ref)
        quadrant(query, kv_ref, slot, which, which, False, False, sums_ref)

    if own:
        quadrant(mine, kv_ref, slot, 0, 1, False, True, sums_ref)
        quadrant(mine, kv_ref, slot, 0, 0, True, True, sums_ref)
        quadrant(mine, kv_ref, slot, 1, 1, True, False, sums_ref)
    else:
        full(mine, i * outer_count + o, False)

    @pl.when(odd == (0 if inner_back == 0 else 1))
    def _():
        full(other, (i + 1 - 2 * odd) * outer_count + o, False)


def own_kernel(off_ref, q_ref, do_ref, rows_ref, qp_ref, dop_ref, rowsp_ref, kv_ref, dq_ref, dqp_ref, sums_ref):
    sums_ref[...] = jnp.zeros_like(sums_ref)
    dqp_ref[...] = jnp.zeros_like(dqp_ref)
    mine = (q_ref, do_ref, rows_ref, dq_ref)
    other = (qp_ref, dop_ref, rowsp_ref, dqp_ref)
    visit(off_ref, mine, other, kv_ref, sums_ref, 0, 0, 0, True)


def store_part(part_ref, sums_ref, slot):
    part_ref[0] = (sums_ref[slot, 0] * SCALE).astype(BF16)
    part_ref[1] = sums_ref[slot, 1].astype(BF16)


def far_kernel(
    off_ref, q_ref, do_ref, rows_ref, qp_ref, dop_ref, rowsp_ref, kv_ref, dq_in, dqp_in, dq_ref, dqp_ref, part_ref, sums_ref
):
    sums_ref[...] = jnp.zeros_like(sums_ref)
    mine = (q_ref, do_ref, rows_ref, dq_ref)
    other = (qp_ref, dop_ref, rowsp_ref, dqp_ref)
    visit(off_ref, mine, other, kv_ref, sums_ref, 0, FAR, BACK, False)
    store_part(part_ref, sums_ref, 0)


def turned(dq_ref, half_at, pair):
    return (dq_ref[half_at, pair] * SCALE).T


def near_kernel(
    off_ref, q_ref, do_ref, rows_ref, qp_ref, dop_ref, rowsp_ref, kvz_ref, kvx_ref, dq_in, dqp_in,
    dq_ref, dqp_ref, partz_ref, partx_ref, pq_ref, sums_ref,
):
    sums_ref[...] = jnp.zeros_like(sums_ref)
    mine = (q_ref, do_ref, rows_ref, dq_ref)
    other = (qp_ref, dop_ref, rowsp_ref, dqp_ref)
    visit(off_ref, mine, other, kvz_ref, sums_ref, 0, 0, BACK, False)
    store_part(partz_ref, sums_ref, 0)
    visit(off_ref, mine, other, kvx_ref, sums_ref, 1, FAR, 0, False)
    store_part(partx_ref, sums_ref, 1)
    half = pq_ref.shape[0] // 2
    for side in range(2):
        for pair in range(dqp_ref.shape[1]):
            block = turned(dqp_ref, side, pair).astype(BF16)
            for j in range(2):
                h = 2 * pair + j
                pq_ref[side * half : (side + 1) * half, h * HEAD_WIDTH : (h + 1) * HEAD_WIDTH] = block[j * half : (j + 1) * half]


def query_kernel(dq_ref, recv_ref, keep_ref, send_ref):
    half = keep_ref.shape[0]
    me = lax.axis_index("head")
    for out_ref, side in ((send_ref, 1 - me), (keep_ref, me)):
        rows = pl.ds(pl.multiple_of(side * half, half), half)
        for pair in range(dq_ref.shape[1]):
            block = turned(dq_ref, side, pair)
            for j in range(2):
                h = 2 * pair + j
                cols = slice(h * HEAD_WIDTH, (h + 1) * HEAD_WIDTH)
                total = block[j * half : (j + 1) * half] + recv_ref[rows, cols].astype(F32)
                out_ref[:, cols] = total.astype(BF16)


def sum_kernel(own_ref, a_ref, b_ref, c_ref, keep_ref, send_ref):
    half = keep_ref.shape[1]
    me = lax.axis_index("head")
    for out_ref, side in ((send_ref, 1 - me), (keep_ref, me)):
        rows = pl.ds(pl.multiple_of(side * half, half), half)
        for at in range(2):
            own = own_ref[0, at, rows, :] * (SCALE if at == 0 else 1.0)
            total = own + a_ref[at, rows, :].astype(F32) + b_ref[at, rows, :].astype(F32) + c_ref[at, rows, :].astype(F32)
            out_ref[at] = total.astype(BF16)


def join_kernel(qk_ref, qr_ref, kk_ref, kr_ref, gq_ref, gk_ref, gv_ref):
    me = lax.axis_index("head")

    def put(out_ref, value, side, width):
        out_ref[0, :, pl.ds(pl.multiple_of(side * width, HEAD_WIDTH), width)] = value

    width = qk_ref.shape[1]
    put(gq_ref, qk_ref[...], me, width)
    put(gq_ref, qr_ref[...], 1 - me, width)
    width = kk_ref.shape[2]
    for at, out_ref in enumerate((gk_ref, gv_ref)):
        put(out_ref, kk_ref[at], me, width)
        put(out_ref, kr_ref[at], 1 - me, width)


def moved(value, inner_steps, outer_steps):
    inner_count, outer_count = lax.axis_size("inner"), lax.axis_size("outer")
    pairs = [
        (i * outer_count + o, (i + inner_steps) % inner_count * outer_count + (o + outer_steps) % outer_count)
        for i in range(inner_count)
        for o in range(outer_count)
    ]
    return lax.ppermute(value, ("inner", "outer"), pairs)


def swapped(value):
    return lax.ppermute(value, "inner", [(i, i ^ 1) for i in range(lax.axis_size("inner"))])


def crossed(value):
    return lax.ppermute(value, "head", [(0, 1), (1, 0)])


def struct(shape, dtype):
    return jax.ShapeDtypeStruct(shape, dtype)


def shards(queries, keys, values, grad_out, log_denominator, output_row_dot, offsets):
    _, tokens, query_cols = queries.shape
    kv_cols = keys.shape[2]
    heads = query_cols // HEAD_WIDTH
    half = tokens // 2
    q, do = queries[0], grad_out[0]
    norm, dots = log_denominator[0].T, output_row_dot[0].T

    kv, rows = call(
        prep_kernel,
        "prep",
        (struct((2, tokens, kv_cols), BF16), struct((2, 2, heads // 2, tokens), F32)),
        [VMEM] * 4,
        bytes_accessed=4 * tokens * kv_cols * 2,
    )(keys[0], values[0], norm, dots)

    kv_far = moved(kv, FAR, BACK)
    kv_back = moved(kv, 0, BACK)
    kv_side = moved(kv, FAR, 0)
    q_other, do_other, rows_other = swapped(q), swapped(do), swapped(rows)

    dq_shape = struct((2, heads // 2, HEAD_WIDTH, tokens), F32)
    part_shape = struct((2, tokens, kv_cols), BF16)
    sums_shape = (1, 2, tokens, kv_cols)
    base = (offsets, q, do, rows, q_other, do_other, rows_other)
    base_specs = [SMEM] + [VMEM] * 6
    flops = 2 * 2 * 5 * heads * tokens * tokens * HEAD_WIDTH

    dq, dq_other, own_sums = call(
        own_kernel, "own", (dq_shape, dq_shape, struct(sums_shape, F32)), base_specs + [VMEM], flops=flops, bytes_accessed=4 << 20
    )(*base, kv)
    dq, dq_other, part_far = call(
        far_kernel,
        "far",
        (dq_shape, dq_shape, part_shape),
        base_specs + [VMEM] * 3,
        flops=flops,
        bytes_accessed=4 << 20,
        aliases={8: 0, 9: 1},
        scratch=[pltpu.VMEM(sums_shape, F32)],
    )(*base, kv_far, dq, dq_other)
    back_far = moved(part_far, -FAR, -BACK)
    dq, dq_other, part_back, part_side, pq = call(
        near_kernel,
        "near",
        (dq_shape, dq_shape, part_shape, part_shape, struct((tokens, query_cols), BF16)),
        base_specs + [VMEM] * 4,
        flops=2 * flops,
        bytes_accessed=4 << 20,
        aliases={9: 0, 10: 1},
        scratch=[pltpu.VMEM((2,) + sums_shape[1:], F32)],
    )(*base, kv_back, kv_side, dq, dq_other)
    back_back = moved(part_back, 0, -BACK)
    back_side = moved(part_side, -FAR, 0)
    pq_other = swapped(pq)
    rows_shape = struct((half, query_cols), BF16)
    q_keep, q_send = call(query_kernel, "query", (rows_shape, rows_shape), [VMEM] * 2, bytes_accessed=2 << 20)(dq, pq_other)
    q_recv = crossed(q_send)
    kv_shape = struct((2, half, kv_cols), BF16)
    kv_keep, kv_send = call(sum_kernel, "sum", (kv_shape, kv_shape), [VMEM] * 4, bytes_accessed=1 << 20)(
        own_sums, back_far, back_back, back_side
    )
    kv_recv = crossed(kv_send)
    return call(
        join_kernel,
        "join",
        (struct((1, half, 2 * query_cols), BF16),) + (struct((1, half, 2 * kv_cols), BF16),) * 2,
        [VMEM] * 4,
        bytes_accessed=2 << 20,
    )(q_keep, q_recv, kv_keep, kv_recv)


def solution(mesh):
    split = P(("inner", "outer"), None, "head")
    joined = P(("inner", "outer"), "head", None)
    return jax.shard_map(
        shards,
        mesh=mesh,
        in_specs=(split,) * 6 + (P(),),
        out_specs=(joined,) * 3,
        check_vma=False,
    )
```

```python
import math

import jax
import jax.numpy as jnp
from jax import lax
from jax.experimental import pallas as pl
from jax.experimental.pallas import tpu as pltpu
from jax.sharding import PartitionSpec as P


HEAD_WIDTH = 128
FAR = 2
BACK = 1

SCALE = 1.0 / math.sqrt(HEAD_WIDTH)
VMEM = pl.BlockSpec(memory_space=pltpu.VMEM)
HBM = pl.BlockSpec(memory_space=pltpu.HBM)
SMEM = pl.BlockSpec(memory_space=pltpu.SMEM)
F32 = jnp.float32
BF16 = jnp.bfloat16
VMEM_LIMIT = 24 * 1024 * 1024


def dot_nt(a, b):
    return lax.dot_general(a, b, (((1,), (1,)), ((), ())), preferred_element_type=F32)


def dot_nn(a, b):
    return lax.dot_general(a, b, (((1,), (0,)), ((), ())), preferred_element_type=F32)


def call(kernel, out_shape, in_specs, *, flops=0, bytes_accessed=0, aliases=None, scratch=(), out_space=None):
    return pl.pallas_call(
        kernel,
        out_shape=out_shape,
        in_specs=in_specs,
        out_specs=jax.tree.map(lambda _: out_space or VMEM, out_shape),
        scratch_shapes=scratch,
        input_output_aliases=aliases or {},
        cost_estimate=pl.CostEstimate(flops=flops, bytes_accessed=bytes_accessed, transcendentals=0),
        compiler_params=pltpu.CompilerParams(vmem_limit_bytes=VMEM_LIMIT),
    )


LOG2E = math.log2(math.e)


def prep_kernel(k_hbm, v_hbm, norm_hbm, dot_hbm, kv_ref, rows_ref, raw_ref, sems):
    copies = [
        pltpu.make_async_copy(source, target, sems.at[at])
        for at, (source, target) in enumerate(
            ((k_hbm, kv_ref.at[0]), (v_hbm, kv_ref.at[1]), (norm_hbm, raw_ref.at[0]), (dot_hbm, raw_ref.at[1]))
        )
    ]
    for copy in copies:
        copy.start()
    for copy in copies:
        copy.wait()
    heads, tokens = raw_ref.shape[1:]
    half = tokens // 2
    lanes = lax.broadcasted_iota(jnp.int32, (heads // 2, tokens), 1)
    for at, factor in enumerate((LOG2E, 1.0)):
        even = raw_ref[at, pl.ds(0, heads // 2, stride=2), :] * factor
        odd = raw_ref[at, pl.ds(1, heads // 2, stride=2), :] * factor
        rows_ref[at, 0] = jnp.where(lanes < half, even, pltpu.roll(odd, half, 1))
        rows_ref[at, 1] = jnp.where(lanes < half, pltpu.roll(even, half, 1), odd)


CHUNK = 4


def half_rows(which, half):
    if isinstance(which, int):
        return pl.ds(which * half, half)
    return pl.ds(pl.multiple_of(which * half, half), half)


def attend(query, g, query_half, blocks, sums_ref, diagonal=False):
    q_ref, do_ref, rows_ref, ds_ref = query
    half = q_ref.shape[0] // 2
    heads_kv = sums_ref.shape[-1] // HEAD_WIDTH
    per_group = q_ref.shape[1] // HEAD_WIDTH // heads_kv
    kv_cols = slice(g * HEAD_WIDTH, (g + 1) * HEAD_WIDTH)
    query_rows = half_rows(query_half, half)
    k = jnp.concatenate([kv_ref[0, half_rows(at, half), kv_cols] for kv_ref, at, _, _ in blocks], 0)
    v = jnp.concatenate([kv_ref[1, half_rows(at, half), kv_cols] for kv_ref, at, _, _ in blocks], 0)
    if diagonal:
        u = lax.broadcasted_iota(jnp.int32, (half, CHUNK * half), 0)
        t = lax.broadcasted_iota(jnp.int32, (half, CHUNK * half), 1) % half
        visible = u <= t
    queries, grads, probs, scores = [], [], [], []
    for c in range(per_group // CHUNK):
        heads = [g * per_group + c * CHUNK + j for j in range(CHUNK)]
        qc = jnp.concatenate([q_ref[query_rows, h * HEAD_WIDTH : (h + 1) * HEAD_WIDTH] for h in heads], 0)
        doc = jnp.concatenate([do_ref[query_rows, h * HEAD_WIDTH : (h + 1) * HEAD_WIDTH] for h in heads], 0)
        pairs = [heads[0] // 2 + i for i in range(CHUNK // 2)]
        norm = jnp.concatenate([rows_ref[0, query_half, pl.ds(p, 1), :] for p in pairs], 1)
        dots = jnp.concatenate([rows_ref[1, query_half, pl.ds(p, 1), :] for p in pairs], 1)
        prob = jnp.exp2(dot_nt(k, qc) * (SCALE * LOG2E) - norm)
        if diagonal:
            prob = jnp.where(visible, prob, 0.0)
        queries.append(qc)
        grads.append(doc)
        probs.append(prob.astype(BF16))
        scores.append((prob * (dot_nt(v, doc) - dots)).astype(BF16))
    score = jnp.concatenate(scores, 1)
    dv = dot_nn(jnp.concatenate(probs, 1), jnp.concatenate(grads, 0))
    dk = dot_nn(score, jnp.concatenate(queries, 0))
    width = score.shape[1]
    for at, (_, key_half, slot, score_slot) in enumerate(blocks):
        mine = slice(at * half, (at + 1) * half)
        sums_ref[slot, 0, half_rows(key_half, half), kv_cols] += dk[mine]
        sums_ref[slot, 1, half_rows(key_half, half), kv_cols] += dv[mine]
        ds_ref[score_slot, :, g * width : (g + 1) * width] = score[mine]


def wrapped(index, steps, count):
    moved = index - steps
    return jnp.where(moved < 0, moved + count, moved)


def block_of(inner_back, outer_back):
    inner_count, outer_count = lax.axis_size("inner"), lax.axis_size("outer")
    inner = wrapped(lax.axis_index("inner"), inner_back, inner_count)
    return inner * outer_count + wrapped(lax.axis_index("outer"), outer_back, outer_count)


def partner_block():
    i = lax.axis_index("inner")
    return (i + 1 - 2 * (i & 1)) * lax.axis_size("outer") + lax.axis_index("outer")


def is_odd():
    return lax.axis_index("inner") & 1


def visit(query, kv_ref, side, slot, sums_ref, sums_slot):
    ds_ref = query[3]
    slots = ds_ref.shape[0] // 3
    ds_ref[(2 - side) * slots + slot] = jnp.zeros(ds_ref.shape[1:], ds_ref.dtype)
    for g in range(sums_ref.shape[-1] // HEAD_WIDTH):
        attend(query, g, 1, [(kv_ref, 0, sums_slot, slot)], sums_ref)
        attend(query, g, side, [(kv_ref, side, sums_slot, (1 + side) * slots + slot)], sums_ref)


SIDE, BACK_SELF, FAR_SELF, OTHER_FIRST, OTHER_SECOND = range(5)


def write_flags(flags_ref, off_ref):
    odd = is_odd()
    own, other = block_of(0, 0), partner_block()
    side, back, far = block_of(FAR, 0), block_of(0, BACK), block_of(FAR, BACK)
    pairs = (
        (side, own),
        (back, own),
        (far, own),
        (jnp.where(odd == 1, side, back), other),
        (jnp.where(odd == 1, far, own), other),
    )
    for row, (keys, queries) in enumerate(pairs):
        flag = jnp.where(off_ref[0, keys] < off_ref[0, queries], 0, 1)
        flags_ref[pl.ds(row, 1), :] = jnp.full((1, flags_ref.shape[1]), flag, jnp.int32)


def flag_of(flags_ref, row):
    return jnp.max(flags_ref[pl.ds(row, 1), :])


def own_kernel(off_hbm, q_hbm, do_hbm, rows_ref, kv_ref, q_ref, do_ref, flags_ref, ds_ref, sums_ref, off_ref, off_sem, sems):
    groups = kv_ref.shape[-1] // HEAD_WIDTH
    width = q_ref.shape[1] // groups
    copies = [
        [
            pltpu.make_async_copy(
                source.at[:, g * width : (g + 1) * width], target.at[:, g * width : (g + 1) * width], sems.at[at, g]
            )
            for at, (source, target) in enumerate(((q_hbm, q_ref), (do_hbm, do_ref)))
        ]
        for g in range(groups)
    ]
    for pair in copies:
        for copy in pair:
            copy.start()
    offsets = pltpu.make_async_copy(off_hbm, off_ref, off_sem)
    offsets.start()
    sums_ref[...] = jnp.zeros_like(sums_ref)
    mine = (q_ref, do_ref, rows_ref, ds_ref)
    slots = ds_ref.shape[0] // 3
    for g in range(groups):
        for copy in copies[g]:
            copy.wait()
        attend(mine, g, 1, [(kv_ref, 0, 0, 0)], sums_ref)
        attend(mine, g, 0, [(kv_ref, 0, 0, slots)], sums_ref, diagonal=True)
        attend(mine, g, 1, [(kv_ref, 1, 0, 2 * slots)], sums_ref, diagonal=True)
    offsets.wait()
    write_flags(flags_ref, off_ref)


def store_part(part_ref, sums_ref, slot):
    part_ref[0] = (sums_ref[slot, 0] * SCALE).astype(BF16)
    part_ref[1] = sums_ref[slot, 1].astype(BF16)


def side_kernel(flags_ref, q_ref, do_ref, rows_ref, kv_ref, ds_in, ds_ref, sums_ref):
    sums_ref[...] = jnp.zeros_like(sums_ref)
    visit((q_ref, do_ref, rows_ref, ds_ref), kv_ref, flag_of(flags_ref, SIDE), 1, sums_ref, 0)


def back_kernel(
    flags_ref, q_ref, do_ref, rows_ref, qp_ref, dop_ref, rowsp_ref, side_ref, kv_ref, side_sums, ds_in,
    ds_ref, dsp_ref, parts_ref, partb_ref, keys_ref, sums_ref,
):
    sums_ref[0] = jnp.zeros(sums_ref.shape[1:], F32)
    sums_ref[1] = side_sums[0]
    odd = is_odd()
    keys_ref[...] = jnp.where(odd == 1, side_ref[...], kv_ref[...])
    visit((q_ref, do_ref, rows_ref, ds_ref), kv_ref, flag_of(flags_ref, BACK_SELF), 2, sums_ref, 0)
    visit((qp_ref, dop_ref, rowsp_ref, dsp_ref), keys_ref, flag_of(flags_ref, OTHER_FIRST), 0, sums_ref, odd)
    store_part(partb_ref, sums_ref, 0)
    store_part(parts_ref, sums_ref, 1)


def query_grads(ds_ref, early_keys, late_keys, put):
    slots = ds_ref.shape[0] // 3
    half = ds_ref.shape[1]
    groups = early_keys.shape[-1] // HEAD_WIDTH
    width = ds_ref.shape[2] // groups
    for g in range(groups):
        cols = slice(g * HEAD_WIDTH, (g + 1) * HEAD_WIDTH)
        early, late = early_keys[:, cols], late_keys[:, cols]
        both = jnp.concatenate([early, late], 0).T

        def scores(region):
            return ds_ref[region * slots : (region + 1) * slots, :, g * width : (g + 1) * width].reshape(slots * half, width)

        for side in range(2):
            if side == 0:
                total = dot_nn(both[:, : slots * half], scores(1))
            else:
                total = dot_nn(both, jnp.concatenate([scores(0), scores(2)], 0))
            total = total * SCALE
            for pair in range(width // (2 * half)):
                block = total[:, pair * 2 * half : (pair + 1) * 2 * half].T
                head = (g * width // half) + 2 * pair
                for j in range(2):
                    put(side, head + j, block[j * half : (j + 1) * half])


def stacked(kvs, half):
    return [jnp.concatenate([kv[0, side * half : (side + 1) * half, :] for kv in kvs], 0) for side in range(2)]


def far_kernel(
    flags_ref, q_ref, do_ref, rows_ref, qp_ref, dop_ref, rowsp_ref, own_ref, kv_ref, first_ref, own_sums, ds_in, dsp_in,
    ds_ref, dsp_ref, owns_ref, part_ref, pq_ref, keys_ref, sums_ref,
):
    sums_ref[0] = jnp.zeros(sums_ref.shape[1:], F32)
    sums_ref[1] = own_sums[0]
    odd = is_odd()
    half = ds_ref.shape[1]
    keys_ref[...] = jnp.where(odd == 1, kv_ref[...], own_ref[...])
    visit((qp_ref, dop_ref, rowsp_ref, dsp_ref), keys_ref, flag_of(flags_ref, OTHER_SECOND), 1, sums_ref, 1 - odd)
    visit((q_ref, do_ref, rows_ref, ds_ref), kv_ref, flag_of(flags_ref, FAR_SELF), 3, sums_ref, 0)
    store_part(part_ref, sums_ref, 0)
    owns_ref[...] = sums_ref[1]
    early, late = stacked([first_ref, keys_ref], half)

    def put(side, head, block):
        pq_ref[side * half : (side + 1) * half, head * HEAD_WIDTH : (head + 1) * HEAD_WIDTH] = block.astype(BF16)

    query_grads(dsp_ref, early, late, put)


def mine_kernel(ds_ref, own_ref, side_ref, back_ref, far_ref, mine_ref):
    half = ds_ref.shape[1]
    early, late = stacked([own_ref, side_ref, back_ref, far_ref], half)

    def put(side, head, block):
        mine_ref[side, :, head * HEAD_WIDTH : (head + 1) * HEAD_WIDTH] = block

    query_grads(ds_ref, early, late, put)


def query_kernel(mine_ref, recv_ref, keep_ref, send_ref):
    half = keep_ref.shape[0]
    me = lax.axis_index("head")
    for out_ref, side in ((send_ref, 1 - me), (keep_ref, me)):
        out_ref[...] = (mine_ref[side] + recv_ref[half_rows(side, half), :].astype(F32)).astype(BF16)


def sum_kernel(own_ref, a_ref, b_ref, c_ref, keep_ref, send_ref):
    half = keep_ref.shape[1]
    me = lax.axis_index("head")
    for out_ref, side in ((send_ref, 1 - me), (keep_ref, me)):
        rows = pl.ds(pl.multiple_of(side * half, half), half)
        for at in range(2):
            own = own_ref[at, rows, :] * (SCALE if at == 0 else 1.0)
            total = own + a_ref[at, rows, :].astype(F32) + b_ref[at, rows, :].astype(F32) + c_ref[at, rows, :].astype(F32)
            out_ref[at] = total.astype(BF16)


def join_kernel(sems, *pairs):
    me = lax.axis_index("head")
    copies = []
    for at, (kept, received, joined) in enumerate(pairs):
        width = kept.shape[-1]
        for j, (source, side) in enumerate(((kept, me), (received, 1 - me))):
            cols = pl.ds(pl.multiple_of(side * width, HEAD_WIDTH), width)
            copies.append(pltpu.make_async_copy(source, joined.at[0, :, cols], sems.at[at, j]))
    for copy in copies:
        copy.start()
    for copy in copies:
        copy.wait()


def join_query_kernel(kept, received, joined, sems):
    join_kernel(sems, (kept, received, joined))


def join_keys_kernel(kept, received, joined_k, joined_v, sems):
    join_kernel(sems, (kept.at[0], received.at[0], joined_k), (kept.at[1], received.at[1], joined_v))


def moved(value, inner_steps, outer_steps):
    inner_count, outer_count = lax.axis_size("inner"), lax.axis_size("outer")
    pairs = [
        (i * outer_count + o, (i + inner_steps) % inner_count * outer_count + (o + outer_steps) % outer_count)
        for i in range(inner_count)
        for o in range(outer_count)
    ]
    return lax.ppermute(value, ("inner", "outer"), pairs)


def swapped(value):
    return lax.ppermute(value, "inner", [(i, i ^ 1) for i in range(lax.axis_size("inner"))])


def crossed(value):
    return lax.ppermute(value, "head", [(0, 1), (1, 0)])


def in_hbm(value):
    return pltpu.with_memory_space_constraint(value, pltpu.HBM)


def struct(shape, dtype):
    return jax.ShapeDtypeStruct(shape, dtype)


def program(queries, keys, values, grad_out, log_denominator, output_row_dot, offsets):
    _, tokens, query_cols = queries.shape
    kv_cols = keys.shape[2]
    heads = query_cols // HEAD_WIDTH
    half = tokens // 2
    q, do = queries[0], grad_out[0]
    norm, dots = log_denominator[0].T, output_row_dot[0].T

    kv, rows = call(
        prep_kernel,
        (struct((2, tokens, kv_cols), BF16), struct((2, 2, heads // 2, tokens), F32)),
        [HBM] * 4,
        bytes_accessed=4 * tokens * kv_cols * 2,
        scratch=[pltpu.VMEM((2, heads, tokens), F32), pltpu.SemaphoreType.DMA((4,))],
    )(*(in_hbm(x) for x in (keys[0], values[0], norm, dots)))

    kv_back = moved(kv, 0, BACK)
    kv_side = moved(kv, FAR, 0)
    kv_far = moved(kv_back, FAR, 0)
    q_other, do_other, rows_other = swapped(q), swapped(do), swapped(rows)

    block_shape = struct((tokens, query_cols), BF16)
    ds_shape = struct((12, half, heads * half), BF16)
    dsp_shape = struct((6, half, heads * half), BF16)
    part_shape = struct((2, tokens, kv_cols), BF16)
    sums_shape = (1, 2, tokens, kv_cols)
    flags_shape = struct((8, tokens), jnp.int32)
    one_sum, two_sums = struct(sums_shape, F32), pltpu.VMEM((2,) + sums_shape[1:], F32)
    keys_scratch = pltpu.VMEM((2, tokens, kv_cols), BF16)
    flops = 2 * 5 * heads * tokens * tokens * HEAD_WIDTH

    q, do, flags, ds, own_sums = call(
        own_kernel,
        (block_shape, block_shape, flags_shape, ds_shape, one_sum),
        [HBM] * 3 + [VMEM] * 2,
        flops=flops,
        bytes_accessed=4 << 20,
        scratch=[
            pltpu.SMEM(offsets.shape[::-1], jnp.int32),
            pltpu.SemaphoreType.DMA,
            pltpu.SemaphoreType.DMA((2, kv_cols // HEAD_WIDTH)),
        ],
    )(in_hbm(offsets.T), in_hbm(q), in_hbm(do), rows, kv)
    mine = (flags, q, do, rows)
    other = (q_other, do_other, rows_other)
    ds, side_sums = call(
        side_kernel, (ds_shape, one_sum), [VMEM] * 6, flops=flops, bytes_accessed=4 << 20, aliases={5: 0}
    )(*mine, kv_side, ds)
    ds, ds_other, part_side, part_back, first_keys = call(
        back_kernel,
        (ds_shape, dsp_shape, part_shape, part_shape, part_shape),
        [VMEM] * 11,
        flops=flops,
        bytes_accessed=4 << 20,
        aliases={10: 0},
        scratch=[two_sums],
    )(*mine, *other, kv_side, kv_back, side_sums, ds)
    ds, ds_other, own_sums, part_far, pq = call(
        far_kernel,
        (ds_shape, dsp_shape, struct(sums_shape[1:], F32), part_shape, block_shape),
        [VMEM] * 13,
        flops=flops,
        bytes_accessed=4 << 20,
        aliases={11: 0, 12: 1},
        scratch=[keys_scratch, two_sums],
    )(*mine, *other, kv, kv_far, first_keys, own_sums, ds, ds_other)
    kvs = (kv, kv_side, kv_back, kv_far)
    back_side = moved(part_side, -FAR, 0)
    back_back = moved(part_back, 0, -BACK)
    pq_other = swapped(pq)
    back_far = moved(part_far, -FAR, -BACK)
    q_mine = call(mine_kernel, struct((2, half, query_cols), F32), [VMEM] * 5, flops=flops // 4, bytes_accessed=1 << 20)(
        ds, *kvs
    )
    rows_shape = struct((half, query_cols), BF16)
    q_keep, q_send = call(query_kernel, (rows_shape, rows_shape), [VMEM] * 2, bytes_accessed=2 << 20)(q_mine, pq_other)
    q_recv = crossed(q_send)
    kv_shape = struct((2, half, kv_cols), BF16)
    kv_keep, kv_send = call(sum_kernel, (kv_shape, kv_shape), [VMEM] * 4, bytes_accessed=1 << 20)(
        own_sums, back_far, back_back, back_side
    )
    kv_recv = crossed(kv_send)
    grad_query = call(
        join_query_kernel,
        struct((1, half, 2 * query_cols), BF16),
        [VMEM] * 2,
        out_space=HBM,
        bytes_accessed=2 << 20,
        scratch=[pltpu.SemaphoreType.DMA((1, 2))],
    )(q_keep, q_recv)
    grad_key, grad_value = call(
        join_keys_kernel,
        (struct((1, half, 2 * kv_cols), BF16),) * 2,
        [VMEM] * 2,
        out_space=HBM,
        bytes_accessed=1 << 18,
        scratch=[pltpu.SemaphoreType.DMA((2, 2))],
    )(kv_keep, kv_recv)
    return grad_query, grad_key, grad_value


def solution(mesh):
    split = P(("inner", "outer"), None, "head")
    joined = P(("inner", "outer"), "head", None)
    return jax.shard_map(
        program,
        mesh=mesh,
        in_specs=(split,) * 6 + (P(),),
        out_specs=(joined,) * 3,
        check_vma=False,
    )
```
